32 devices in a mesh: cases: 2 (over y), runs: 16 (over z, x, core).
Axes of the slice: x: 2, y: 2, z: 4, core: 2. Of those that a mesh axis runs over, the one named last changes fastest.
Arguments:
- run_inputs: float32 [2048, 24], P(('cases', 'runs')), parts along dimension 0, may hold values from -3 to 3
- term_codes: int32 [4096, 4], replicated, may hold values from 0 to 119
- weight_levels: int32 [4096], replicated, may hold values from 0 to 3
- correlations: bfloat16 [8192, 1024], P(('cases', 'runs')), parts along dimension 0, may hold values from -32 to 32
- slab_modes: bfloat16 [4096, 1024], P('cases'), parts along dimension 0, may hold values from -0.1875 to 0.1875
- cell_map: int32 [2048], replicated, may hold values from 0 to 2047, each once
Outputs:
- coefficients: float32 [8192, 1024], P(('cases', 'runs')), parts along dimension 0
- lifted: bfloat16 [8192, 2048], P(('cases', 'runs')), parts along dimension 0
The draws below stay inside these ranges and needn't reach their ends.
There are 2 independent parts, one for each index of `cases`. The reference program is written for one: setup_inputs(seed, part) draws one part's arguments, and reference() takes and returns one part's arrays. A program takes and returns all parts, laid end to end along the dimension named above; an argument that names none is the same for every part. Nothing has to cross between parts.
All inputs are finite; a program needn't handle non-finite values.
Results may differ from the reference program's by a relative error of at most 0.0067.
Values may be sent and summed in bfloat16 or wider, within the bound.
A program may use at most 64 MiB of HBM per device.

```python
import math
import jax
import jax.numpy as jnp
from jax import lax

P_SIZE = 4096
M = 1024
DIM = 24
SLOTS = 4
RUN_DEV = 64
CELLS = 2048
RUNS = 1024
CODES = 120
N_RUNS = 16


def draw_correlations(key, part):
    keys = jax.random.split(key, 3)
    row_scale = jnp.exp(jax.random.uniform(keys[0], (P_SIZE, 1), minval=jnp.log(0.3), maxval=jnp.log(3.0)))
    column_scale = jnp.exp(jax.random.uniform(keys[2], (1, M), minval=jnp.log(0.5), maxval=jnp.log(2.0)))
    noise = jnp.clip(jax.random.normal(keys[1], (P_SIZE, M)), -4.0, 4.0)
    values = row_scale * column_scale * noise
    return values.astype(jnp.float32).astype(jnp.bfloat16)


def set_ends(entries, key, smallest, top_value):
    longest = entries.shape.index(max(entries.shape))
    spots = []
    for shift in (0, 1):
        where = [jax.random.randint(jax.random.fold_in(key, axis), (), 0, length) for axis, length in enumerate(entries.shape)]
        where[longest] = (where[longest] + shift) % entries.shape[longest]
        spots.append(tuple(where))
    return entries.at[spots[0]].set(smallest).at[spots[1]].set(top_value)


def shard_levels(rng, dims, cuts, low, largest):
    level = 1.0
    for position, shards_of in cuts:
        draws = jax.random.uniform(jax.random.fold_in(jax.random.fold_in(rng, 6), position), (shards_of,), jnp.float32, low / len(cuts), largest / len(cuts))
        level = level * jnp.repeat(jnp.exp(draws), dims[position] // shards_of).reshape((-1,) + (1,) * (len(dims) - 1 - position))
    return level


def gaussian(key, shape, spread, most, shards=(), dtype=jnp.bfloat16):
    drawn = spread * jax.random.normal(key, shape, jnp.float32)
    if shards:
        drawn = drawn * shard_levels(key, shape, shards, -0.22, 0.18)
    return jnp.clip(drawn, -most, most).astype(dtype)


def setup_inputs(seed: int = 0, part: int = 0) -> dict:
    key_list = jax.random.split(jax.random.key(seed), 7)
    own_keys = jax.random.split(jax.random.fold_in(key_list[6], part), 7)
    run_inputs = gaussian(own_keys[0], (RUNS, DIM), 1.0, 3.0, ((0, 16),), jnp.float32)
    term_codes = set_ends(jax.random.randint(key_list[1], (P_SIZE, SLOTS), 0, CODES), jax.random.fold_in(key_list[1], 1), 0, CODES - 1).astype(jnp.int32)
    weight_levels = set_ends(jax.random.randint(key_list[2], (P_SIZE,), 0, 4), jax.random.fold_in(key_list[2], 1), 0, 3).astype(jnp.int32)
    correlations = draw_correlations(jax.random.fold_in(jax.random.fold_in(key_list[6], part), 71), part)
    slab_modes = gaussian(own_keys[4], (CELLS, M), M ** -0.5, 0.1875)
    cell_map = jax.random.permutation(key_list[5], CELLS).astype(jnp.int32)
    return {"run_inputs": run_inputs, "term_codes": term_codes, "weight_levels": weight_levels, "correlations": correlations, "slab_modes": slab_modes, "cell_map": cell_map}


STEP = 0.5
LAMBDA_FRACTION = 0.05
EPSILON = 1e-06
ROOT_TWO = math.sqrt(2.0)
ROOT_SIX = math.sqrt(6.0)
ROOT_TWENTYFOUR = math.sqrt(24.0)

def hermite_table(points):
    squared = points * points
    columns = [jnp.ones_like(points), points, (squared - 1.0) / ROOT_TWO, points * (squared - 3.0) / ROOT_SIX, (squared * squared - 6.0 * squared + 3.0) / ROOT_TWENTYFOUR]
    return jnp.stack(columns, axis=-1).reshape(points.shape[0], -1)

def basis(points, codes):
    hermite = hermite_table(points)
    product = jnp.take(hermite, codes[:, 0], axis=1)
    for column in range(1, codes.shape[1]):
        product = product * jnp.take(hermite, codes[:, column], axis=1)
    return product.astype(jnp.bfloat16)

def shrink(values, limits):
    length = jnp.sqrt(lax.optimization_barrier(jnp.sum(values * values, axis=1, keepdims=True)) + EPSILON)
    return values * jnp.maximum(0.0, 1.0 - limits[:, None] / length)

def reference(run_inputs, term_codes, weight_levels, correlations, slab_modes, cell_map):
    weights = jnp.exp2(weight_levels.astype(jnp.float32))
    corr = correlations.astype(jnp.float32)
    penalty = LAMBDA_FRACTION * jnp.max(jnp.sqrt(lax.optimization_barrier(jnp.sum(corr * corr, axis=1))) / weights)
    first = shrink(STEP * corr, STEP * penalty * weights)
    first_wide = first.astype(jnp.bfloat16).astype(jnp.float32)
    blocks = run_inputs.reshape(N_RUNS, RUN_DEV, DIM)

    def accumulate(running, points):
        design = basis(points, term_codes).astype(jnp.float32)
        fitted = jnp.dot(design, first_wide, preferred_element_type=jnp.float32).astype(jnp.bfloat16)
        return (running + jnp.dot(design.T, fitted.astype(jnp.float32), preferred_element_type=jnp.float32), None)
    summed, _ = lax.scan(accumulate, jnp.zeros((P_SIZE, M), jnp.float32), blocks)
    gradient = summed / RUNS - corr
    coefficients = shrink(first - STEP * gradient, STEP * penalty * weights)
    modes = jnp.take(slab_modes, cell_map, axis=0).astype(jnp.float32)
    coeff_wide = coefficients.astype(jnp.bfloat16).astype(jnp.float32)
    lifted = jnp.dot(coeff_wide, modes.T, preferred_element_type=jnp.float32).astype(jnp.bfloat16)
    return (coefficients, lifted)
```

```python
import functools
import math

import jax
import jax.numpy as jnp
from jax import lax
from jax.experimental import pallas as pl
from jax.experimental.pallas import tpu as pltpu
from jax.sharding import PartitionSpec as P

STEP = 0.5
LAMBDA_FRACTION = 0.05
EPSILON = 1e-06
ROOT_TWO = math.sqrt(2.0)
ROOT_SIX = math.sqrt(6.0)
ROOT_TWENTYFOUR = math.sqrt(24.0)
DEGREES = 5
LANES = 128


def hermite_columns(points):
    squared = points * points
    return [
        jnp.ones_like(points),
        points,
        (squared - 1.0) / ROOT_TWO,
        points * (squared - 3.0) / ROOT_SIX,
        (squared * squared - 6.0 * squared + 3.0) / ROOT_TWENTYFOUR,
    ]


def hermite_table(points):
    return jnp.stack(hermite_columns(points), axis=-1).reshape(points.shape[0], -1)


def basis(points, codes):
    hermite = hermite_table(points)
    product = jnp.take(hermite, codes[:, 0], axis=1)
    for column in range(1, codes.shape[1]):
        product = product * jnp.take(hermite, codes[:, column], axis=1)
    return product.astype(jnp.bfloat16)


def shrink(values, limits):
    length = jnp.sqrt(jnp.sum(values * values, axis=1, keepdims=True) + EPSILON)
    return values * jnp.maximum(0.0, 1.0 - limits / length)


def dot_nn(left, right):
    return lax.dot_general(
        left, right, (((1,), (0,)), ((), ())), preferred_element_type=jnp.float32
    )


def dot_nt(left, right):
    return lax.dot_general(
        left, right, (((1,), (1,)), ((), ())), preferred_element_type=jnp.float32
    )


def kernel(
    n,
    corr_hbm,
    points_hbm,
    levels_hbm,
    codes_hbm,
    map_hbm,
    slab_hbm,
    coef_ref,
    permuted,
    points_all,
    norms_all,
    corr_ref,
    points_ref,
    levels_ref,
    codes_ref,
    map_ref,
    weights,
    blocks,
    table,
    design,
    total,
    total_in,
    fitted,
    outgoing,
    summed,
    codes,
    cells,
    slab,
    local_sem,
    points_send,
    points_recv,
    norms_send,
    norms_recv,
    relay_send,
    relay_recv,
    blocks_send,
    blocks_recv,
    total_send,
    total_recv,
    summed_send,
    summed_recv,
):
    me = lax.axis_index("runs")
    chips = n // 2
    chip = me // 2
    core = lax.rem(me, 2)
    terms, modes = corr_ref.shape
    width = modes // chips
    runs = table.shape[1]
    half = table.shape[0] // 2
    side = chips // 2
    low_side = chip < side
    inner = jnp.logical_and(chip >= side // 2, chip < chips - side // 2)

    def peer(offset):
        return lax.rem(me + offset, n)

    def chip_at(offset):
        return lax.rem(chip + offset, chips)

    def near_chip(step):
        base = chip // side * side
        return base + lax.rem(chip - base + step, side)

    def far_chip(step):
        row = step // 2
        row = jnp.where(low_side, side - 1 - row, row)
        return 2 * row + lax.rem(chip + 1 + step, 2)

    def offset_to(there):
        return lax.rem(there - chip + chips, chips)

    def term_rows(index):
        return pl.ds(pl.multiple_of(index * terms, terms), terms)

    def mode_lanes(index):
        return pl.ds(pl.multiple_of(index * width, width), width)

    def remote(src, dst, send, recv, target):
        return pltpu.make_async_remote_copy(
            src_ref=src,
            dst_ref=dst,
            send_sem=send,
            recv_sem=recv,
            device_id={"runs": target},
            device_id_type=pl.DeviceIdType.MESH,
        )

    barrier = pltpu.get_barrier_semaphore()
    for offset in range(1, n):
        pl.semaphore_signal(
            barrier,
            inc=1,
            device_id={"runs": peer(offset)},
            device_id_type=pl.DeviceIdType.MESH,
        )

    copies = [
        pltpu.make_async_copy(src, dst, local_sem.at[index])
        for index, (src, dst) in enumerate(
            [
                (corr_hbm, corr_ref),
                (points_hbm, points_ref),
                (levels_hbm, levels_ref),
                (codes_hbm, codes_ref),
                (map_hbm, map_ref),
                (slab_hbm, slab),
            ]
        )
    ]
    slab_copy = copies[-1]
    own_copy = pltpu.make_async_copy(
        corr_ref.at[:, mode_lanes(chip)],
        blocks.at[term_rows(chip)],
        local_sem.at[len(copies)],
    )
    for copy in copies:
        copy.start()
    for copy in copies[:2]:
        copy.wait()
    own_copy.start()

    wide = corr_ref[...].astype(jnp.float32)
    squares = wide * wide
    high = squares.astype(jnp.bfloat16)
    low = (squares - high.astype(jnp.float32)).astype(jnp.bfloat16)
    ones = jnp.ones((8, modes), jnp.bfloat16)
    norm_rows = dot_nt(ones, high) + dot_nt(ones, low)
    norms_all[core, chip] = norm_rows[0:1]
    raw = points_ref[...]
    inputs = raw.shape[0]
    points_all[core, chip] = jnp.concatenate(
        [jnp.where(core == side, raw, 0.0) for side in range(2)], axis=1
    )
    pl.semaphore_wait(barrier, n - 1)

    def points_move(offset):
        return remote(
            points_all.at[core, chip],
            points_all.at[core, chip],
            points_send.at[offset],
            points_recv.at[offset],
            chip_at(offset) * 2 + core,
        )

    def norms_move(offset):
        return remote(
            norms_all.at[core, chip],
            norms_all.at[core, chip],
            norms_send.at[offset],
            norms_recv.at[offset],
            chip_at(offset) * 2 + core,
        )

    def block_move(offset):
        there = chip_at(offset)
        return remote(
            corr_ref.at[:, mode_lanes(there)],
            blocks.at[term_rows(chip)],
            blocks_send.at[offset],
            blocks_recv.at[offset],
            there * 2 + core,
        )

    def relays():
        other = chip * 2 + (1 - core)
        mine, norms = points_all.at[core], norms_all.at[core]
        return (
            remote(mine, mine, relay_send.at[0], relay_recv.at[0], other),
            remote(norms, norms, relay_send.at[1], relay_recv.at[1], other),
        )

    def total_move():
        return remote(total, total_in, total_send, total_recv, chip * 2 + (1 - core))

    def summed_move(offset):
        there = chip_at(offset)
        return remote(
            outgoing.at[term_rows(there)],
            summed.at[:, mode_lanes(chip)],
            summed_send.at[offset],
            summed_recv.at[offset],
            there * 2 + core,
        )

    targets = [far_chip(step) for step in range(side)]
    targets += [near_chip(step) for step in range(1, side)]
    for there in targets:
        points_move(offset_to(there)).start()
    for there in targets:
        norms_move(offset_to(there)).start()
    def send_far():
        for step in range(side):
            block_move(offset_to(far_chip(step))).start()

    pl.when(inner)(send_far)
    for step in range(1, side):
        block_move(offset_to(near_chip(step))).start()

    for copy in copies[2:-1]:
        copy.wait()
    for index in range(n):
        weights[index % 2, index // 2] = jnp.exp2(
            levels_ref[index].astype(jnp.float32)
        )

    for index in range(chips):
        lanes = term_rows(index * 2 + core)
        code = codes_ref[:, lanes]
        position = lax.shift_right_logical(code * 205, 10)
        code = (code - DEGREES * position) * inputs + position
        spare = jnp.zeros((8 - code.shape[0], terms), jnp.int32)
        codes[index * terms : (index + 1) * terms, :] = jnp.transpose(
            jnp.concatenate([code, spare], axis=0)
        )

    for start in range(0, map_ref.shape[1], 256):
        lanes = slice(start, start + 256)
        cells[lanes, :] = jnp.transpose(
            jnp.broadcast_to(map_ref[:, lanes], (8, 256))
        )

    pl.when(jnp.logical_not(inner))(send_far)

    place = lax.broadcasted_iota(jnp.int32, (256, slab.shape[0]), 1)
    chunks = cells.shape[0] // 256
    early, middle = chunks // 4, 3 * chunks // 8

    def permute(first, last):
        @pl.loop(first, last)
        def _(step):
            rows = pl.ds(pl.multiple_of(step * 256, 256), 256)
            pick = jnp.where(place == cells[rows, 0:1], 1.0, 0.0).astype(jnp.bfloat16)
            permuted[rows, :] = dot_nn(pick, slab[...]).astype(jnp.bfloat16)

    slab_copy.wait()
    permute(0, early)
    for offset in range(1, chips):
        points_move(offset).wait_recv()
        norms_move(offset).wait_recv()
    points_relay, norms_relay = relays()
    points_relay.start()
    norms_relay.start()
    permute(early, middle)
    points_relay.wait_recv()
    norms_relay.wait_recv()
    for index in range(chips):
        points = points_all[0, index] + points_all[1, index]
        columns = hermite_columns(points)
        used = DEGREES * points.shape[0]
        if used < half:
            columns.append(jnp.zeros((half - used, points.shape[1]), jnp.float32))
        values = jnp.concatenate(columns, axis=0)
        upper = values.astype(jnp.bfloat16)
        lower = (values - upper.astype(jnp.float32)).astype(jnp.bfloat16)
        lanes = slice(index * points.shape[1], (index + 1) * points.shape[1])
        table[0:half, lanes] = upper
        table[half:, lanes] = lower

    ratio = jnp.sqrt(norms_all[...]) / weights[...]
    penalty = LAMBDA_FRACTION * jnp.max(
        jnp.max(jnp.max(ratio, axis=0), axis=0), axis=1, keepdims=True
    )
    own_copy.wait()
    total[...] = jnp.zeros_like(total)
    position = lax.broadcasted_iota(jnp.int32, (terms, 2 * half), 1)
    position = jnp.where(position >= half, position - half, position)
    piece = min(256, runs)

    @pl.loop(0, chips, unroll=2)
    def _(step):
        there = jnp.where(
            step < side, near_chip(step), far_chip(chips - 1 - lax.max(step, side))
        )
        rows = term_rows(there)
        picks = [
            jnp.where(position == codes[rows, slot : slot + 1], 1.0, 0.0).astype(
                jnp.bfloat16
            )
            for slot in range(codes_ref.shape[0])
        ]
        for start in range(0, runs, piece):
            lanes = slice(start, start + piece)
            product = dot_nn(picks[0], table[:, lanes])
            for pick in picks[1:]:
                product = product * dot_nn(pick, table[:, lanes])
            design[rows, lanes] = product.astype(jnp.bfloat16)

        @pl.when(step > 0)
        def _():
            block_move(lax.rem(chip - there + chips, chips)).wait_recv()

        length = jnp.sqrt(STEP * STEP * norms_all[core, there] + EPSILON)
        limits = STEP * penalty * weights[core, there]
        factor = jnp.maximum(0.0, 1.0 - limits / length)
        turned = jnp.transpose(blocks[rows, :].astype(jnp.float32))
        first_half = (STEP * turned * factor).astype(jnp.bfloat16)
        total[...] += dot_nn(first_half, design[rows, :])

    total_move().start()
    total_move().wait_recv()
    fitted[...] = (total[...] + total_in[...]).astype(jnp.bfloat16)

    @pl.loop(1, chips)
    def _(step):
        there = jnp.where(
            step <= side, far_chip(lax.min(step, side) - 1), near_chip(step - side)
        )
        rows = term_rows(there)
        outgoing[rows, :] = dot_nt(design[rows, :], fitted[...]).astype(jnp.bfloat16)
        summed_move(offset_to(there)).start()

    summed[:, mode_lanes(chip)] = dot_nt(
        design[term_rows(chip), :], fitted[...]
    ).astype(jnp.bfloat16)

    permute(middle, chunks)
    own_limits = jnp.broadcast_to(STEP * penalty * weights[core, chip], (8, terms))
    limits = jnp.transpose(own_limits)[:, 0:1]
    corr = corr_ref[...].astype(jnp.float32)
    first = shrink(STEP * corr, limits)
    for offset in range(1, chips):
        summed_move(offset).wait_recv()
    gradient = summed[...].astype(jnp.float32) / runs - corr
    coefficients = shrink(first - STEP * gradient, limits)
    coef_ref[...] = coefficients

    points_relay.wait_send()
    norms_relay.wait_send()
    for offset in range(1, chips):
        points_move(offset).wait_send()
        norms_move(offset).wait_send()
        block_move(offset).wait_send()
        summed_move(offset).wait_send()
    total_move().wait_send()


def finish(coef_in, permuted, coef_ref, lift_ref):
    step = pl.program_id(0)
    rows, width = coef_ref.shape[0], lift_ref.shape[1]
    own = pl.ds(pl.multiple_of(step * rows, rows), rows)
    coef_ref[...] = coef_in[own, :]
    cells = pl.ds(pl.multiple_of(step * width, width), width)
    narrow = coef_in[...].astype(jnp.bfloat16)
    lift_ref[...] = dot_nt(narrow, permuted[cells, :]).astype(jnp.bfloat16)


def by_chips(run_inputs, term_codes, weight_levels, correlations, slab_modes, cell_map):
    run_count, inputs = run_inputs.shape
    terms, modes = correlations.shape
    n = lax.axis_size("runs")
    chips = n // 2
    runs = run_count * n
    count = cell_map.shape[0]
    width = modes // chips
    lane_terms = chips * terms
    half = -(-DEGREES * inputs // LANES) * LANES
    f32, bf16 = jnp.float32, jnp.bfloat16
    vmem = pl.BlockSpec(memory_space=pltpu.VMEM)
    hbm = pl.BlockSpec(memory_space=pltpu.HBM)
    dma = pltpu.SemaphoreType.DMA
    coefficients, permuted = pl.pallas_call(
        functools.partial(kernel, n),
        out_shape=(
            jax.ShapeDtypeStruct((terms, modes), f32),
            jax.ShapeDtypeStruct((count, modes), bf16),
        ),
        in_specs=[hbm] * 6,
        out_specs=(vmem, vmem),
        scratch_shapes=[
            pltpu.VMEM((2, chips, inputs, 2 * run_count), f32),
            pltpu.VMEM((2, chips, 1, terms), f32),
            pltpu.VMEM((terms, modes), bf16),
            pltpu.VMEM((inputs, run_count), f32),
            pltpu.VMEM((n, 1, terms), jnp.int32),
            pltpu.VMEM((term_codes.shape[1], n * terms), jnp.int32),
            pltpu.VMEM((1, count), jnp.int32),
            pltpu.VMEM((2, chips, 1, terms), f32),
            pltpu.VMEM((lane_terms, width), bf16),
            pltpu.VMEM((2 * half, runs), bf16),
            pltpu.VMEM((lane_terms, runs), bf16),
            pltpu.VMEM((width, runs), f32),
            pltpu.VMEM((width, runs), f32),
            pltpu.VMEM((width, runs), bf16),
            pltpu.VMEM((lane_terms, width), bf16),
            pltpu.VMEM((terms, modes), bf16),
            pltpu.VMEM((lane_terms, 8), jnp.int32),
            pltpu.VMEM((count, 8), jnp.int32),
            pltpu.VMEM(slab_modes.shape, bf16),
            dma((7,)),
            dma((chips,)),
            dma((chips,)),
            dma((chips,)),
            dma((chips,)),
            dma((2,)),
            dma((7,)),
            dma((chips,)),
            dma((chips,)),
            dma,
            dma,
            dma((chips,)),
            dma((chips,)),
        ],
        compiler_params=pltpu.CompilerParams(
            collective_id=0, has_side_effects=True, vmem_limit_bytes=40 * 2**20
        ),
    )(
        *[
            pltpu.with_memory_space_constraint(array, pltpu.HBM)
            for array in (
                correlations,
                run_inputs.T,
                weight_levels.reshape(n, 1, terms),
                term_codes.T,
                cell_map.reshape(1, count),
                slab_modes,
            )
        ]
    )
    steps = 4
    return pl.pallas_call(
        finish,
        grid=(steps,),
        out_shape=(
            jax.ShapeDtypeStruct((terms, modes), f32),
            jax.ShapeDtypeStruct((terms, count), bf16),
        ),
        in_specs=[vmem, vmem],
        out_specs=(
            pl.BlockSpec((terms // steps, modes), lambda step: (step, 0)),
            pl.BlockSpec((terms, count // steps), lambda step: (0, step)),
        ),
        compiler_params=pltpu.CompilerParams(vmem_limit_bytes=8 * 2**20),
    )(coefficients, permuted)


def by_gathers(
    run_inputs, term_codes, weight_levels, correlations, slab_modes, cell_map
):
    run_count = run_inputs.shape[0]
    term_count = correlations.shape[0]
    devices = lax.axis_size("runs")
    offset = lax.axis_index("runs") * term_count
    total_runs = run_count * devices
    weights_all = jnp.exp2(weight_levels.astype(jnp.float32))
    own_weights = lax.dynamic_slice_in_dim(weights_all, offset, term_count)
    own_corr = correlations.astype(jnp.float32)
    ratio = jnp.max(jnp.sqrt(jnp.sum(own_corr * own_corr, axis=1)) / own_weights)
    penalty = LAMBDA_FRACTION * lax.pmax(ratio, "runs")
    limits = (STEP * penalty * own_weights)[:, None]
    first = shrink(STEP * own_corr, limits)
    design = basis(run_inputs, term_codes)
    fitted = dot_nn(
        design,
        lax.all_gather(first.astype(jnp.bfloat16), "runs", axis=0, tiled=True),
    )
    fitted_half = fitted.astype(jnp.bfloat16)
    all_points = lax.all_gather(run_inputs, "runs", axis=0, tiled=True)
    own_codes = lax.dynamic_slice_in_dim(term_codes, offset, term_count, 0)
    owned_design = basis(all_points, own_codes)
    summed = lax.dot_general(
        owned_design,
        lax.all_gather(fitted_half, "runs", axis=0, tiled=True),
        (((0,), (0,)), ((), ())),
        preferred_element_type=jnp.float32,
    )
    gradient = summed / total_runs - own_corr
    coefficients = shrink(first - STEP * gradient, limits)
    modes = jnp.take(slab_modes, cell_map, axis=0)
    lifted = dot_nt(coefficients.astype(jnp.bfloat16), modes).astype(jnp.bfloat16)
    return (coefficients, lifted)


def on_device(run_inputs, term_codes, weight_levels, correlations, slab_modes, cell_map):
    n = lax.axis_size("runs")
    terms, modes = correlations.shape
    aligned = (
        n % 8 == 0
        and modes % (LANES * max(n // 2, 1)) == 0
        and terms % LANES == 0
        and term_codes.shape[1] <= 8
        and DEGREES * run_inputs.shape[1] < 1024
        and (2 * run_inputs.shape[0]) % LANES == 0
        and run_inputs.shape[1] % 8 == 0
        and cell_map.shape[0] % 512 == 0
        and (run_inputs.shape[0] * n) % 256 == 0
    )
    step = by_chips if aligned else by_gathers
    return step(
        run_inputs, term_codes, weight_levels, correlations, slab_modes, cell_map
    )


def solution(mesh):
    return jax.shard_map(
        on_device,
        mesh=mesh,
        in_specs=(
            P(("cases", "runs"), None),
            P(),
            P(),
            P(("cases", "runs"), None),
            P("cases", None),
            P(),
        ),
        out_specs=(P(("cases", "runs"), None), P(("cases", "runs"), None)),
        check_vma=False,
    )
```

```python
import functools
import math

import jax
import jax.numpy as jnp
from jax import lax
from jax.experimental import pallas as pl
from jax.experimental.pallas import tpu as pltpu
from jax.sharding import PartitionSpec as P

STEP = 0.5
LAMBDA_FRACTION = 0.05
EPSILON = 1e-06
ROOT_TWO = math.sqrt(2.0)
ROOT_SIX = math.sqrt(6.0)
ROOT_TWENTYFOUR = math.sqrt(24.0)
DEGREES = 5
LANES = 128


def hermite_columns(points):
    squared = points * points
    return [
        jnp.ones_like(points),
        points,
        (squared - 1.0) / ROOT_TWO,
        points * (squared - 3.0) / ROOT_SIX,
        (squared * squared - 6.0 * squared + 3.0) / ROOT_TWENTYFOUR,
    ]


def hermite_table(points):
    return jnp.stack(hermite_columns(points), axis=-1).reshape(points.shape[0], -1)


def basis(points, codes):
    hermite = hermite_table(points)
    product = jnp.take(hermite, codes[:, 0], axis=1)
    for column in range(1, codes.shape[1]):
        product = product * jnp.take(hermite, codes[:, column], axis=1)
    return product.astype(jnp.bfloat16)


def shrink(values, limits):
    length = jnp.sqrt(jnp.sum(values * values, axis=1, keepdims=True) + EPSILON)
    return values * jnp.maximum(0.0, 1.0 - limits / length)


def dot_nn(left, right):
    return lax.dot_general(
        left, right, (((1,), (0,)), ((), ())), preferred_element_type=jnp.float32
    )


def dot_nt(left, right):
    return lax.dot_general(
        left, right, (((1,), (1,)), ((), ())), preferred_element_type=jnp.float32
    )


def kernel(
    n,
    corr_hbm,
    points_hbm,
    levels_hbm,
    codes_hbm,
    map_hbm,
    slab_hbm,
    coef_ref,
    permuted,
    packets,
    norms_all,
    points_all,
    corr_ref,
    points_ref,
    levels_ref,
    codes_ref,
    map_ref,
    weights,
    blocks,
    table,
    design,
    total,
    total_in,
    fitted,
    outgoing,
    summed,
    codes,
    cells,
    slab,
    local_sem,
    packets_send,
    packets_recv,
    relay_send,
    relay_recv,
    blocks_send,
    blocks_recv,
    total_send,
    total_recv,
    summed_send,
    summed_recv,
):
    me = lax.axis_index("runs")
    chips = n // 2
    chip = me // 2
    core = lax.rem(me, 2)
    terms, modes = corr_ref.shape
    width = modes // chips
    runs = table.shape[1]
    half = table.shape[0] // 2
    side = chips // 2
    low_side = chip < side
    inner = jnp.logical_and(chip >= side // 2, chip < chips - side // 2)

    def peer(offset):
        return lax.rem(me + offset, n)

    def chip_at(offset):
        return lax.rem(chip + offset, chips)

    def near_chip(step):
        base = chip // side * side
        return base + lax.rem(chip - base + step, side)

    def far_chip(step):
        row = step // 2
        row = jnp.where(low_side, side - 1 - row, row)
        return 2 * row + lax.rem(chip + 1 + step, 2)

    def offset_to(there):
        return lax.rem(there - chip + chips, chips)

    def term_rows(index):
        return pl.ds(pl.multiple_of(index * terms, terms), terms)

    def mode_lanes(index):
        return pl.ds(pl.multiple_of(index * width, width), width)

    def remote(src, dst, send, recv, target):
        return pltpu.make_async_remote_copy(
            src_ref=src,
            dst_ref=dst,
            send_sem=send,
            recv_sem=recv,
            device_id={"runs": target},
            device_id_type=pl.DeviceIdType.MESH,
        )

    barrier = pltpu.get_barrier_semaphore()
    for offset in range(1, n):
        pl.semaphore_signal(
            barrier,
            inc=1,
            device_id={"runs": peer(offset)},
            device_id_type=pl.DeviceIdType.MESH,
        )

    copies = [
        pltpu.make_async_copy(src, dst, local_sem.at[index])
        for index, (src, dst) in enumerate(
            [
                (corr_hbm, corr_ref),
                (points_hbm, points_ref),
                (levels_hbm, levels_ref),
                (codes_hbm, codes_ref),
                (map_hbm, map_ref),
                (slab_hbm, slab),
            ]
        )
    ]
    slab_copy = copies[-1]
    own_copy = pltpu.make_async_copy(
        corr_ref.at[:, mode_lanes(chip)],
        blocks.at[term_rows(chip)],
        local_sem.at[len(copies)],
    )
    for copy in copies:
        copy.start()
    for copy in copies[:2]:
        copy.wait()
    own_copy.start()

    wide = corr_ref[...].astype(jnp.float32)
    squares = wide * wide
    high = squares.astype(jnp.bfloat16)
    low = (squares - high.astype(jnp.float32)).astype(jnp.bfloat16)
    ones = jnp.ones((8, modes), jnp.bfloat16)
    norm_rows = dot_nt(ones, high) + dot_nt(ones, low)
    inputs = points_ref.shape[0]
    fold = inputs // 2
    norm_lanes = [
        (fold + start // LANES, slice(start, start + LANES))
        for start in range(0, terms, LANES)
    ]
    packets[core, chip, 0:fold] = jnp.concatenate(
        [points_ref[0:fold], points_ref[fold:inputs]], axis=1
    )
    for row, lanes in norm_lanes:
        packets[core, chip, row : row + 1] = norm_rows[0:1, lanes]
    pl.semaphore_wait(barrier, n - 1)

    def packet_move(offset):
        return remote(
            packets.at[core, chip],
            packets.at[core, chip],
            packets_send.at[offset],
            packets_recv.at[offset],
            chip_at(offset) * 2 + core,
        )

    def block_move(offset):
        there = chip_at(offset)
        return remote(
            corr_ref.at[:, mode_lanes(there)],
            blocks.at[term_rows(chip)],
            blocks_send.at[offset],
            blocks_recv.at[offset],
            there * 2 + core,
        )

    def relay():
        mine = packets.at[core]
        return remote(mine, mine, relay_send, relay_recv, chip * 2 + (1 - core))

    def total_move():
        return remote(total, total_in, total_send, total_recv, chip * 2 + (1 - core))

    def summed_move(offset):
        there = chip_at(offset)
        return remote(
            outgoing.at[term_rows(there)],
            summed.at[:, mode_lanes(chip)],
            summed_send.at[offset],
            summed_recv.at[offset],
            there * 2 + core,
        )

    targets = [far_chip(step) for step in range(side)]
    targets += [near_chip(step) for step in range(1, side)]
    for there in targets:
        packet_move(offset_to(there)).start()
    def send_far():
        for step in range(side):
            block_move(offset_to(far_chip(step))).start()

    pl.when(inner)(send_far)
    for step in range(1, side):
        block_move(offset_to(near_chip(step))).start()

    for copy in copies[2:-1]:
        copy.wait()
    for index in range(n):
        weights[index % 2, index // 2] = jnp.exp2(
            levels_ref[index].astype(jnp.float32)
        )

    for index in range(chips):
        lanes = term_rows(index * 2 + core)
        code = codes_ref[:, lanes]
        position = lax.shift_right_logical(code * 205, 10)
        code = (code - DEGREES * position) * inputs + position
        spare = jnp.zeros((8 - code.shape[0], terms), jnp.int32)
        codes[index * terms : (index + 1) * terms, :] = jnp.transpose(
            jnp.concatenate([code, spare], axis=0)
        )

    for start in range(0, map_ref.shape[1], 256):
        lanes = slice(start, start + 256)
        cells[lanes, :] = jnp.transpose(
            jnp.broadcast_to(map_ref[:, lanes], (8, 256))
        )

    pl.when(jnp.logical_not(inner))(send_far)

    place = lax.broadcasted_iota(jnp.int32, (256, slab.shape[0]), 1)
    chunks = cells.shape[0] // 256
    early, middle = chunks // 4, 3 * chunks // 8

    def permute(first, last):
        @pl.loop(first, last)
        def _(step):
            rows = pl.ds(pl.multiple_of(step * 256, 256), 256)
            pick = jnp.where(place == cells[rows, 0:1], 1.0, 0.0).astype(jnp.bfloat16)
            permuted[rows, :] = dot_nn(pick, slab[...]).astype(jnp.bfloat16)

    slab_copy.wait()
    permute(0, early)
    for offset in range(1, chips):
        packet_move(offset).wait_recv()
    packets_relay = relay()
    packets_relay.start()
    permute(early, middle)
    packets_relay.wait_recv()
    first_core = lax.broadcasted_iota(jnp.int32, (fold, LANES), 1) < LANES // 2
    for index in range(chips):
        even, odd = (packets[side, index, 0:fold] for side in range(2))
        turned = pltpu.roll(odd, LANES // 2, 1)
        points_all[index, 0:fold] = jnp.where(first_core, even, turned)
        turned = pltpu.roll(even, LANES // 2, 1)
        points_all[index, fold:inputs] = jnp.where(first_core, turned, odd)
        for which in range(2):
            for row, lanes in norm_lanes:
                norms_all[which, index, :, lanes] = packets[which, index, row : row + 1]
    for index in range(chips):
        points = points_all[index]
        columns = hermite_columns(points)
        used = DEGREES * points.shape[0]
        if used < half:
            columns.append(jnp.zeros((half - used, points.shape[1]), jnp.float32))
        values = jnp.concatenate(columns, axis=0)
        upper = values.astype(jnp.bfloat16)
        lower = (values - upper.astype(jnp.float32)).astype(jnp.bfloat16)
        lanes = slice(index * points.shape[1], (index + 1) * points.shape[1])
        table[0:half, lanes] = upper
        table[half:, lanes] = lower

    ratio = jnp.sqrt(norms_all[...]) / weights[...]
    penalty = LAMBDA_FRACTION * jnp.max(
        jnp.max(jnp.max(ratio, axis=0), axis=0), axis=1, keepdims=True
    )
    own_copy.wait()
    total[...] = jnp.zeros_like(total)
    position = lax.broadcasted_iota(jnp.int32, (terms, 2 * half), 1)
    position = jnp.where(position >= half, position - half, position)
    piece = min(256, runs)

    def build(there):
        rows = term_rows(there)
        picks = [
            jnp.where(position == codes[rows, slot : slot + 1], 1.0, 0.0).astype(
                jnp.bfloat16
            )
            for slot in range(codes_ref.shape[0])
        ]
        for start in range(0, runs, piece):
            lanes = slice(start, start + piece)
            product = dot_nn(picks[0], table[:, lanes])
            for pick in picks[1:]:
                product = product * dot_nn(pick, table[:, lanes])
            design[rows, lanes] = product.astype(jnp.bfloat16)

    def fit(there):
        rows = term_rows(there)
        length = jnp.sqrt(STEP * STEP * norms_all[core, there] + EPSILON)
        limits = STEP * penalty * weights[core, there]
        factor = jnp.maximum(0.0, 1.0 - limits / length)
        turned = jnp.transpose(blocks[rows, :].astype(jnp.float32))
        first_half = (STEP * turned * factor).astype(jnp.bfloat16)
        total[...] += dot_nn(first_half, design[rows, :])

    def wait_block(there):
        block_move(lax.rem(chip - there + chips, chips)).wait_recv()

    @pl.loop(0, side, unroll=2)
    def _(step):
        there = near_chip(step)
        build(there)
        pl.when(step > 0)(lambda: wait_block(there))
        fit(there)

    @pl.loop(0, side, unroll=2)
    def _(step):
        build(far_chip(step))

    for step in range(side):
        wait_block(far_chip(side - 1 - step))
        fit(far_chip(side - 1 - step))

    total_move().start()
    total_move().wait_recv()
    fitted[...] = (total[...] + total_in[...]).astype(jnp.bfloat16)

    @pl.loop(1, chips)
    def _(step):
        there = jnp.where(
            step <= side, far_chip(lax.min(step, side) - 1), near_chip(step - side)
        )
        rows = term_rows(there)
        outgoing[rows, :] = dot_nt(design[rows, :], fitted[...]).astype(jnp.bfloat16)
        summed_move(offset_to(there)).start()

    summed[:, mode_lanes(chip)] = dot_nt(
        design[term_rows(chip), :], fitted[...]
    ).astype(jnp.bfloat16)

    permute(middle, chunks)
    own_limits = jnp.broadcast_to(STEP * penalty * weights[core, chip], (8, terms))
    limits = jnp.transpose(own_limits)[:, 0:1]
    chunk = 32
    for start in range(0, terms, chunk):
        rows = slice(start, start + chunk)
        half_corr = STEP * corr_ref[rows].astype(jnp.float32)
        coef_ref[rows] = shrink(half_corr, limits[rows]) + half_corr
    for offset in range(1, chips):
        summed_move(offset).wait_recv()
    for start in range(0, terms, chunk):
        rows = slice(start, start + chunk)
        step_sum = summed[rows].astype(jnp.float32) * (STEP / runs)
        coef_ref[rows] = shrink(coef_ref[rows] - step_sum, limits[rows])

    packets_relay.wait_send()
    for offset in range(1, chips):
        packet_move(offset).wait_send()
        block_move(offset).wait_send()
        summed_move(offset).wait_send()
    total_move().wait_send()


def finish(coef_in, permuted, coef_ref, lift_ref):
    step = pl.program_id(0)
    rows, width = coef_ref.shape[0], lift_ref.shape[1]
    own = pl.ds(pl.multiple_of(step * rows, rows), rows)
    coef_ref[...] = coef_in[own, :]
    cells = pl.ds(pl.multiple_of(step * width, width), width)
    narrow = coef_in[...].astype(jnp.bfloat16)
    lift_ref[...] = dot_nt(narrow, permuted[cells, :]).astype(jnp.bfloat16)


def by_chips(run_inputs, term_codes, weight_levels, correlations, slab_modes, cell_map):
    run_count, inputs = run_inputs.shape
    terms, modes = correlations.shape
    n = lax.axis_size("runs")
    chips = n // 2
    runs = run_count * n
    count = cell_map.shape[0]
    width = modes // chips
    lane_terms = chips * terms
    packet = -(-(inputs // 2 + terms // LANES) // 8) * 8
    half = -(-DEGREES * inputs // LANES) * LANES
    f32, bf16 = jnp.float32, jnp.bfloat16
    vmem = pl.BlockSpec(memory_space=pltpu.VMEM)
    hbm = pl.BlockSpec(memory_space=pltpu.HBM)
    dma = pltpu.SemaphoreType.DMA
    coefficients, permuted = pl.pallas_call(
        functools.partial(kernel, n),
        out_shape=(
            jax.ShapeDtypeStruct((terms, modes), f32),
            jax.ShapeDtypeStruct((count, modes), bf16),
        ),
        in_specs=[hbm] * 6,
        out_specs=(vmem, vmem),
        scratch_shapes=[
            pltpu.VMEM((2, chips, packet, LANES), f32),
            pltpu.VMEM((2, chips, 1, terms), f32),
            pltpu.VMEM((chips, inputs, LANES), f32),
            pltpu.VMEM((terms, modes), bf16),
            pltpu.VMEM((inputs, run_count), f32),
            pltpu.VMEM((n, 1, terms), jnp.int32),
            pltpu.VMEM((term_codes.shape[1], n * terms), jnp.int32),
            pltpu.VMEM((1, count), jnp.int32),
            pltpu.VMEM((2, chips, 1, terms), f32),
            pltpu.VMEM((lane_terms, width), bf16),
            pltpu.VMEM((2 * half, runs), bf16),
            pltpu.VMEM((lane_terms, runs), bf16),
            pltpu.VMEM((width, runs), f32),
            pltpu.VMEM((width, runs), f32),
            pltpu.VMEM((width, runs), bf16),
            pltpu.VMEM((lane_terms, width), bf16),
            pltpu.VMEM((terms, modes), bf16),
            pltpu.VMEM((lane_terms, 8), jnp.int32),
            pltpu.VMEM((count, 8), jnp.int32),
            pltpu.VMEM(slab_modes.shape, bf16),
            dma((7,)),
            dma((chips,)),
            dma((chips,)),
            dma,
            dma,
            dma((chips,)),
            dma((chips,)),
            dma,
            dma,
            dma((chips,)),
            dma((chips,)),
        ],
        compiler_params=pltpu.CompilerParams(
            collective_id=0, has_side_effects=True, vmem_limit_bytes=40 * 2**20
        ),
    )(
        *[
            pltpu.with_memory_space_constraint(array, pltpu.HBM)
            for array in (
                correlations,
                run_inputs.T,
                weight_levels.reshape(n, 1, terms),
                term_codes.T,
                cell_map.reshape(1, count),
                slab_modes,
            )
        ]
    )
    steps = 4
    return pl.pallas_call(
        finish,
        grid=(steps,),
        out_shape=(
            jax.ShapeDtypeStruct((terms, modes), f32),
            jax.ShapeDtypeStruct((terms, count), bf16),
        ),
        in_specs=[vmem, vmem],
        out_specs=(
            pl.BlockSpec((terms // steps, modes), lambda step: (step, 0)),
            pl.BlockSpec((terms, count // steps), lambda step: (0, step)),
        ),
        compiler_params=pltpu.CompilerParams(vmem_limit_bytes=8 * 2**20),
    )(coefficients, permuted)


def by_gathers(
    run_inputs, term_codes, weight_levels, correlations, slab_modes, cell_map
):
    run_count = run_inputs.shape[0]
    term_count = correlations.shape[0]
    devices = lax.axis_size("runs")
    offset = lax.axis_index("runs") * term_count
    total_runs = run_count * devices
    weights_all = jnp.exp2(weight_levels.astype(jnp.float32))
    own_weights = lax.dynamic_slice_in_dim(weights_all, offset, term_count)
    own_corr = correlations.astype(jnp.float32)
    ratio = jnp.max(jnp.sqrt(jnp.sum(own_corr * own_corr, axis=1)) / own_weights)
    penalty = LAMBDA_FRACTION * lax.pmax(ratio, "runs")
    limits = (STEP * penalty * own_weights)[:, None]
    first = shrink(STEP * own_corr, limits)
    design = basis(run_inputs, term_codes)
    fitted = dot_nn(
        design,
        lax.all_gather(first.astype(jnp.bfloat16), "runs", axis=0, tiled=True),
    )
    fitted_half = fitted.astype(jnp.bfloat16)
    all_points = lax.all_gather(run_inputs, "runs", axis=0, tiled=True)
    own_codes = lax.dynamic_slice_in_dim(term_codes, offset, term_count, 0)
    owned_design = basis(all_points, own_codes)
    summed = lax.dot_general(
        owned_design,
        lax.all_gather(fitted_half, "runs", axis=0, tiled=True),
        (((0,), (0,)), ((), ())),
        preferred_element_type=jnp.float32,
    )
    gradient = summed / total_runs - own_corr
    coefficients = shrink(first - STEP * gradient, limits)
    modes = jnp.take(slab_modes, cell_map, axis=0)
    lifted = dot_nt(coefficients.astype(jnp.bfloat16), modes).astype(jnp.bfloat16)
    return (coefficients, lifted)


def on_device(run_inputs, term_codes, weight_levels, correlations, slab_modes, cell_map):
    n = lax.axis_size("runs")
    terms, modes = correlations.shape
    aligned = (
        n % 8 == 0
        and modes % (LANES * max(n // 2, 1)) == 0
        and terms % LANES == 0
        and term_codes.shape[1] <= 8
        and DEGREES * run_inputs.shape[1] < 1024
        and 2 * run_inputs.shape[0] == LANES
        and run_inputs.shape[1] % 8 == 0
        and cell_map.shape[0] % 512 == 0
        and (run_inputs.shape[0] * n) % 256 == 0
    )
    step = by_chips if aligned else by_gathers
    return step(
        run_inputs, term_codes, weight_levels, correlations, slab_modes, cell_map
    )


def solution(mesh):
    return jax.shard_map(
        on_device,
        mesh=mesh,
        in_specs=(
            P(("cases", "runs"), None),
            P(),
            P(),
            P(("cases", "runs"), None),
            P("cases", None),
            P(),
        ),
        out_specs=(P(("cases", "runs"), None), P(("cases", "runs"), None)),
        check_vma=False,
    )
```

```python
import functools
import math

import jax
import jax.numpy as jnp
from jax import lax
from jax.experimental import pallas as pl
from jax.experimental.pallas import tpu as pltpu
from jax.sharding import PartitionSpec as P

STEP = 0.5
LAMBDA_FRACTION = 0.05
EPSILON = 1e-06
ROOT_TWO = math.sqrt(2.0)
ROOT_SIX = math.sqrt(6.0)
ROOT_TWENTYFOUR = math.sqrt(24.0)
DEGREES = 5
LANES = 128


def hermite_columns(points):
    squared = points * points
    return [
        jnp.ones_like(points),
        points,
        (squared - 1.0) / ROOT_TWO,
        points * (squared - 3.0) / ROOT_SIX,
        (squared * squared - 6.0 * squared + 3.0) / ROOT_TWENTYFOUR,
    ]


def hermite_table(points):
    return jnp.stack(hermite_columns(points), axis=-1).reshape(points.shape[0], -1)


def basis(points, codes):
    hermite = hermite_table(points)
    product = jnp.take(hermite, codes[:, 0], axis=1)
    for column in range(1, codes.shape[1]):
        product = product * jnp.take(hermite, codes[:, column], axis=1)
    return product.astype(jnp.bfloat16)


def shrink(values, limits):
    length = jnp.sqrt(jnp.sum(values * values, axis=1, keepdims=True) + EPSILON)
    return values * jnp.maximum(0.0, 1.0 - limits / length)


def dot_nn(left, right):
    return lax.dot_general(
        left, right, (((1,), (0,)), ((), ())), preferred_element_type=jnp.float32
    )


def dot_nt(left, right):
    return lax.dot_general(
        left, right, (((1,), (1,)), ((), ())), preferred_element_type=jnp.float32
    )


def kernel(
    n,
    corr_hbm,
    points_hbm,
    levels_hbm,
    codes_hbm,
    map_hbm,
    slab_hbm,
    coef_ref,
    narrow_ref,
    permuted,
    packets,
    norms_all,
    points_all,
    corr_ref,
    points_ref,
    levels_ref,
    codes_ref,
    map_ref,
    weights,
    blocks,
    table,
    design,
    total,
    total_in,
    fitted,
    outgoing,
    summed,
    codes,
    cells,
    slab,
    local_sem,
    packets_send,
    packets_recv,
    relay_send,
    relay_recv,
    blocks_send,
    blocks_recv,
    total_send,
    total_recv,
    summed_send,
    summed_recv,
):
    me = lax.axis_index("runs")
    chips = n // 2
    chip = me // 2
    core = lax.rem(me, 2)
    terms, modes = corr_ref.shape
    width = modes // chips
    runs = table.shape[1]
    half = table.shape[0] // 2
    side = chips // 2
    low_side = chip < side
    inner = jnp.logical_and(chip >= side // 2, chip < chips - side // 2)

    def peer(offset):
        return lax.rem(me + offset, n)

    def chip_at(offset):
        return lax.rem(chip + offset, chips)

    def near_chip(step):
        base = chip // side * side
        return base + lax.rem(chip - base + step, side)

    def far_chip(step):
        row = step // 2
        row = jnp.where(low_side, side - 1 - row, row)
        return 2 * row + lax.rem(chip + 1 + step, 2)

    def offset_to(there):
        return lax.rem(there - chip + chips, chips)

    def term_rows(index):
        return pl.ds(pl.multiple_of(index * terms, terms), terms)

    def mode_lanes(index):
        return pl.ds(pl.multiple_of(index * width, width), width)

    def remote(src, dst, send, recv, target):
        return pltpu.make_async_remote_copy(
            src_ref=src,
            dst_ref=dst,
            send_sem=send,
            recv_sem=recv,
            device_id={"runs": target},
            device_id_type=pl.DeviceIdType.MESH,
        )

    barrier = pltpu.get_barrier_semaphore()
    for offset in range(1, n):
        pl.semaphore_signal(
            barrier,
            inc=1,
            device_id={"runs": peer(offset)},
            device_id_type=pl.DeviceIdType.MESH,
        )

    copies = [
        pltpu.make_async_copy(src, dst, local_sem.at[index])
        for index, (src, dst) in enumerate(
            [
                (corr_hbm, corr_ref),
                (points_hbm, points_ref),
                (levels_hbm, levels_ref),
                (codes_hbm, codes_ref),
                (map_hbm, map_ref),
                (slab_hbm, slab),
            ]
        )
    ]
    slab_copy = copies[-1]
    own_copy = pltpu.make_async_copy(
        corr_ref.at[:, mode_lanes(chip)],
        blocks.at[term_rows(chip)],
        local_sem.at[len(copies)],
    )
    for copy in copies:
        copy.start()
    for copy in copies[:2]:
        copy.wait()
    own_copy.start()

    wide = corr_ref[...].astype(jnp.float32)
    squares = wide * wide
    high = squares.astype(jnp.bfloat16)
    low = (squares - high.astype(jnp.float32)).astype(jnp.bfloat16)
    ones = jnp.ones((8, modes), jnp.bfloat16)
    norm_rows = dot_nt(ones, high) + dot_nt(ones, low)
    inputs = points_ref.shape[0]
    fold = inputs // 2
    norm_lanes = [
        (fold + start // LANES, slice(start, start + LANES))
        for start in range(0, terms, LANES)
    ]
    packets[core, chip, 0:fold] = jnp.concatenate(
        [points_ref[0:fold], points_ref[fold:inputs]], axis=1
    )
    for row, lanes in norm_lanes:
        packets[core, chip, row : row + 1] = norm_rows[0:1, lanes]
    pl.semaphore_wait(barrier, n - 1)

    def packet_move(offset):
        return remote(
            packets.at[core, chip],
            packets.at[core, chip],
            packets_send.at[offset],
            packets_recv.at[offset],
            chip_at(offset) * 2 + core,
        )

    def block_move(offset):
        there = chip_at(offset)
        return remote(
            corr_ref.at[:, mode_lanes(there)],
            blocks.at[term_rows(chip)],
            blocks_send.at[offset],
            blocks_recv.at[offset],
            there * 2 + core,
        )

    def relay():
        mine = packets.at[core]
        return remote(mine, mine, relay_send, relay_recv, chip * 2 + (1 - core))

    def total_move():
        return remote(total, total_in, total_send, total_recv, chip * 2 + (1 - core))

    def summed_move(offset):
        there = chip_at(offset)
        return remote(
            outgoing.at[term_rows(there)],
            summed.at[:, mode_lanes(chip)],
            summed_send.at[offset],
            summed_recv.at[offset],
            there * 2 + core,
        )

    targets = [far_chip(step) for step in range(side)]
    targets += [near_chip(step) for step in range(1, side)]
    for there in targets:
        packet_move(offset_to(there)).start()
    def send_far():
        for step in range(side):
            block_move(offset_to(far_chip(step))).start()

    pl.when(inner)(send_far)
    for step in range(1, side):
        block_move(offset_to(near_chip(step))).start()

    for copy in copies[2:-1]:
        copy.wait()
    for index in range(n):
        weights[index % 2, index // 2] = jnp.exp2(
            levels_ref[index].astype(jnp.float32)
        )

    for index in range(chips):
        lanes = term_rows(index * 2 + core)
        code = codes_ref[:, lanes]
        position = lax.shift_right_logical(code * 205, 10)
        code = (code - DEGREES * position) * inputs + position
        spare = jnp.zeros((8 - code.shape[0], terms), jnp.int32)
        codes[index * terms : (index + 1) * terms, :] = jnp.transpose(
            jnp.concatenate([code, spare], axis=0)
        )

    for start in range(0, map_ref.shape[1], 256):
        lanes = slice(start, start + 256)
        cells[lanes, :] = jnp.transpose(
            jnp.broadcast_to(map_ref[:, lanes], (8, 256))
        )

    pl.when(jnp.logical_not(inner))(send_far)

    place = lax.broadcasted_iota(jnp.int32, (256, slab.shape[0]), 1)
    chunks = cells.shape[0] // 256
    early, middle = chunks // 8, chunks // 4

    def permute(first, last):
        @pl.loop(first, last)
        def _(step):
            rows = pl.ds(pl.multiple_of(step * 256, 256), 256)
            pick = jnp.where(place == cells[rows, 0:1], 1.0, 0.0).astype(jnp.bfloat16)
            permuted[rows, :] = dot_nn(pick, slab[...]).astype(jnp.bfloat16)

    slab_copy.wait()
    permute(0, early)
    for offset in range(1, chips):
        packet_move(offset).wait_recv()
    packets_relay = relay()
    packets_relay.start()
    permute(early, middle)
    packets_relay.wait_recv()
    first_core = lax.broadcasted_iota(jnp.int32, (fold, LANES), 1) < LANES // 2
    for index in range(chips):
        even, odd = (packets[side, index, 0:fold] for side in range(2))
        turned = pltpu.roll(odd, LANES // 2, 1)
        points_all[index, 0:fold] = jnp.where(first_core, even, turned)
        turned = pltpu.roll(even, LANES // 2, 1)
        points_all[index, fold:inputs] = jnp.where(first_core, turned, odd)
        for which in range(2):
            for row, lanes in norm_lanes:
                norms_all[which, index, :, lanes] = packets[which, index, row : row + 1]
    for index in range(chips):
        points = points_all[index]
        columns = hermite_columns(points)
        used = DEGREES * points.shape[0]
        if used < half:
            columns.append(jnp.zeros((half - used, points.shape[1]), jnp.float32))
        values = jnp.concatenate(columns, axis=0)
        upper = values.astype(jnp.bfloat16)
        lower = (values - upper.astype(jnp.float32)).astype(jnp.bfloat16)
        lanes = slice(index * points.shape[1], (index + 1) * points.shape[1])
        table[0:half, lanes] = upper
        table[half:, lanes] = lower

    ratio = jnp.sqrt(norms_all[...]) / weights[...]
    penalty = LAMBDA_FRACTION * jnp.max(
        jnp.max(jnp.max(ratio, axis=0), axis=0), axis=1, keepdims=True
    )
    own_copy.wait()
    total[...] = jnp.zeros_like(total)
    position = lax.broadcasted_iota(jnp.int32, (terms, 2 * half), 1)
    position = jnp.where(position >= half, position - half, position)
    piece = min(256, runs)

    def build(there):
        rows = term_rows(there)
        picks = [
            jnp.where(position == codes[rows, slot : slot + 1], 1.0, 0.0).astype(
                jnp.bfloat16
            )
            for slot in range(codes_ref.shape[0])
        ]
        for start in range(0, runs, piece):
            lanes = slice(start, start + piece)
            product = dot_nn(picks[0], table[:, lanes])
            for pick in picks[1:]:
                product = product * dot_nn(pick, table[:, lanes])
            design[rows, lanes] = product.astype(jnp.bfloat16)

    def fit(there):
        rows = term_rows(there)
        length = jnp.sqrt(STEP * STEP * norms_all[core, there] + EPSILON)
        limits = STEP * penalty * weights[core, there]
        factor = jnp.maximum(0.0, 1.0 - limits / length)
        turned = jnp.transpose(blocks[rows, :].astype(jnp.float32))
        first_half = (STEP * turned * factor).astype(jnp.bfloat16)
        total[...] += dot_nn(first_half, design[rows, :])

    def wait_block(there):
        block_move(lax.rem(chip - there + chips, chips)).wait_recv()

    @pl.loop(0, chips, unroll=2)
    def _(step):
        build(step)

    fit(chip)
    for step in range(1, side):
        wait_block(near_chip(step))
        fit(near_chip(step))
    for step in range(side):
        wait_block(far_chip(side - 1 - step))
        fit(far_chip(side - 1 - step))

    total_move().start()
    total_move().wait_recv()
    fitted[...] = (total[...] + total_in[...]).astype(jnp.bfloat16)

    @pl.loop(1, chips)
    def _(step):
        there = jnp.where(
            step <= side, far_chip(lax.min(step, side) - 1), near_chip(step - side)
        )
        rows = term_rows(there)
        outgoing[rows, :] = dot_nt(design[rows, :], fitted[...]).astype(jnp.bfloat16)
        summed_move(offset_to(there)).start()

    summed[:, mode_lanes(chip)] = dot_nt(
        design[term_rows(chip), :], fitted[...]
    ).astype(jnp.bfloat16)

    permute(middle, chunks)
    own_limits = jnp.broadcast_to(STEP * penalty * weights[core, chip], (8, terms))
    limits = jnp.transpose(own_limits)[:, 0:1]
    chunk = 32
    for start in range(0, terms, chunk):
        rows = slice(start, start + chunk)
        half_corr = STEP * corr_ref[rows].astype(jnp.float32)
        coef_ref[rows] = shrink(half_corr, limits[rows]) + half_corr
    for offset in range(1, chips):
        summed_move(offset).wait_recv()
    for start in range(0, terms, chunk):
        rows = slice(start, start + chunk)
        step_sum = summed[rows].astype(jnp.float32) * (STEP / runs)
        coefficients = shrink(coef_ref[rows] - step_sum, limits[rows])
        coef_ref[rows] = coefficients
        narrow_ref[rows] = coefficients.astype(jnp.bfloat16)

    packets_relay.wait_send()
    for offset in range(1, chips):
        packet_move(offset).wait_send()
        block_move(offset).wait_send()
        summed_move(offset).wait_send()
    total_move().wait_send()


def finish(coef_in, narrow, permuted, coef_hbm, lift_hbm, lift, sems):
    copies = [pltpu.make_async_copy(coef_in, coef_hbm, sems.at[0])]
    copies[0].start()
    parts, _, width = lift.shape
    for part in range(parts):
        lanes = slice(part * width, (part + 1) * width)
        lift[part] = dot_nt(narrow[...], permuted[lanes]).astype(jnp.bfloat16)
        copy = pltpu.make_async_copy(
            lift.at[part], lift_hbm.at[:, lanes], sems.at[part + 1]
        )
        copy.start()
        copies.append(copy)
    for copy in copies:
        copy.wait()


def by_chips(run_inputs, term_codes, weight_levels, correlations, slab_modes, cell_map):
    run_count, inputs = run_inputs.shape
    terms, modes = correlations.shape
    n = lax.axis_size("runs")
    chips = n // 2
    runs = run_count * n
    count = cell_map.shape[0]
    width = modes // chips
    lane_terms = chips * terms
    packet = -(-(inputs // 2 + terms // LANES) // 8) * 8
    half = -(-DEGREES * inputs // LANES) * LANES
    f32, bf16 = jnp.float32, jnp.bfloat16
    vmem = pl.BlockSpec(memory_space=pltpu.VMEM)
    hbm = pl.BlockSpec(memory_space=pltpu.HBM)
    dma = pltpu.SemaphoreType.DMA
    *solved, permuted = pl.pallas_call(
        functools.partial(kernel, n),
        out_shape=(
            jax.ShapeDtypeStruct((terms, modes), f32),
            jax.ShapeDtypeStruct((terms, modes), bf16),
            jax.ShapeDtypeStruct((count, modes), bf16),
        ),
        in_specs=[hbm] * 6,
        out_specs=(vmem, vmem, vmem),
        scratch_shapes=[
            pltpu.VMEM((2, chips, packet, LANES), f32),
            pltpu.VMEM((2, chips, 1, terms), f32),
            pltpu.VMEM((chips, inputs, LANES), f32),
            pltpu.VMEM((terms, modes), bf16),
            pltpu.VMEM((inputs, run_count), f32),
            pltpu.VMEM((n, 1, terms), jnp.int32),
            pltpu.VMEM((term_codes.shape[1], n * terms), jnp.int32),
            pltpu.VMEM((1, count), jnp.int32),
            pltpu.VMEM((2, chips, 1, terms), f32),
            pltpu.VMEM((lane_terms, width), bf16),
            pltpu.VMEM((2 * half, runs), bf16),
            pltpu.VMEM((lane_terms, runs), bf16),
            pltpu.VMEM((width, runs), f32),
            pltpu.VMEM((width, runs), f32),
            pltpu.VMEM((width, runs), bf16),
            pltpu.VMEM((lane_terms, width), bf16),
            pltpu.VMEM((terms, modes), bf16),
            pltpu.VMEM((lane_terms, 8), jnp.int32),
            pltpu.VMEM((count, 8), jnp.int32),
            pltpu.VMEM(slab_modes.shape, bf16),
            dma((7,)),
            dma((chips,)),
            dma((chips,)),
            dma,
            dma,
            dma((chips,)),
            dma((chips,)),
            dma,
            dma,
            dma((chips,)),
            dma((chips,)),
        ],
        compiler_params=pltpu.CompilerParams(
            collective_id=0, has_side_effects=True, vmem_limit_bytes=40 * 2**20
        ),
    )(
        *[
            pltpu.with_memory_space_constraint(array, pltpu.HBM)
            for array in (
                correlations,
                run_inputs.T,
                weight_levels.reshape(n, 1, terms),
                term_codes.T,
                cell_map.reshape(1, count),
                slab_modes,
            )
        ]
    )
    width = 256
    parts = count // width
    return pl.pallas_call(
        finish,
        out_shape=(
            jax.ShapeDtypeStruct((terms, modes), f32),
            jax.ShapeDtypeStruct((terms, count), bf16),
        ),
        in_specs=[vmem, vmem, vmem],
        out_specs=(hbm, hbm),
        scratch_shapes=[
            pltpu.VMEM((parts, terms, width), bf16),
            dma((parts + 1,)),
        ],
        compiler_params=pltpu.CompilerParams(vmem_limit_bytes=8 * 2**20),
    )(*solved, permuted)


def by_gathers(
    run_inputs, term_codes, weight_levels, correlations, slab_modes, cell_map
):
    run_count = run_inputs.shape[0]
    term_count = correlations.shape[0]
    devices = lax.axis_size("runs")
    offset = lax.axis_index("runs") * term_count
    total_runs = run_count * devices
    weights_all = jnp.exp2(weight_levels.astype(jnp.float32))
    own_weights = lax.dynamic_slice_in_dim(weights_all, offset, term_count)
    own_corr = correlations.astype(jnp.float32)
    ratio = jnp.max(jnp.sqrt(jnp.sum(own_corr * own_corr, axis=1)) / own_weights)
    penalty = LAMBDA_FRACTION * lax.pmax(ratio, "runs")
    limits = (STEP * penalty * own_weights)[:, None]
    first = shrink(STEP * own_corr, limits)
    design = basis(run_inputs, term_codes)
    fitted = dot_nn(
        design,
        lax.all_gather(first.astype(jnp.bfloat16), "runs", axis=0, tiled=True),
    )
    fitted_half = fitted.astype(jnp.bfloat16)
    all_points = lax.all_gather(run_inputs, "runs", axis=0, tiled=True)
    own_codes = lax.dynamic_slice_in_dim(term_codes, offset, term_count, 0)
    owned_design = basis(all_points, own_codes)
    summed = lax.dot_general(
        owned_design,
        lax.all_gather(fitted_half, "runs", axis=0, tiled=True),
        (((0,), (0,)), ((), ())),
        preferred_element_type=jnp.float32,
    )
    gradient = summed / total_runs - own_corr
    coefficients = shrink(first - STEP * gradient, limits)
    modes = jnp.take(slab_modes, cell_map, axis=0)
    lifted = dot_nt(coefficients.astype(jnp.bfloat16), modes).astype(jnp.bfloat16)
    return (coefficients, lifted)


def on_device(run_inputs, term_codes, weight_levels, correlations, slab_modes, cell_map):
    n = lax.axis_size("runs")
    terms, modes = correlations.shape
    aligned = (
        n % 8 == 0
        and modes % (LANES * max(n // 2, 1)) == 0
        and terms % LANES == 0
        and term_codes.shape[1] <= 8
        and DEGREES * run_inputs.shape[1] < 1024
        and 2 * run_inputs.shape[0] == LANES
        and run_inputs.shape[1] % 8 == 0
        and cell_map.shape[0] % 512 == 0
        and (run_inputs.shape[0] * n) % 256 == 0
    )
    step = by_chips if aligned else by_gathers
    return step(
        run_inputs, term_codes, weight_levels, correlations, slab_modes, cell_map
    )


def solution(mesh):
    return jax.shard_map(
        on_device,
        mesh=mesh,
        in_specs=(
            P(("cases", "runs"), None),
            P(),
            P(),
            P(("cases", "runs"), None),
            P("cases", None),
            P(),
        ),
        out_specs=(P(("cases", "runs"), None), P(("cases", "runs"), None)),
        check_vma=False,
    )
```

```python
import functools
import math

import jax
import jax.numpy as jnp
from jax import lax
from jax.experimental import pallas as pl
from jax.experimental.pallas import tpu as pltpu
from jax.sharding import PartitionSpec as P

STEP = 0.5
LAMBDA_FRACTION = 0.05
EPSILON = 1e-06
ROOT_TWO = math.sqrt(2.0)
ROOT_SIX = math.sqrt(6.0)
ROOT_TWENTYFOUR = math.sqrt(24.0)
DEGREES = 5
LANES = 128


def hermite_columns(points):
    squared = points * points
    return [
        jnp.ones_like(points),
        points,
        (squared - 1.0) / ROOT_TWO,
        points * (squared - 3.0) / ROOT_SIX,
        (squared * squared - 6.0 * squared + 3.0) / ROOT_TWENTYFOUR,
    ]


def hermite_table(points):
    return jnp.stack(hermite_columns(points), axis=-1).reshape(points.shape[0], -1)


def basis(points, codes):
    hermite = hermite_table(points)
    product = jnp.take(hermite, codes[:, 0], axis=1)
    for column in range(1, codes.shape[1]):
        product = product * jnp.take(hermite, codes[:, column], axis=1)
    return product.astype(jnp.bfloat16)


def shrink(values, limits):
    length = jnp.sqrt(jnp.sum(values * values, axis=1, keepdims=True) + EPSILON)
    return values * jnp.maximum(0.0, 1.0 - limits / length)


def dot_nn(left, right):
    return lax.dot_general(
        left, right, (((1,), (0,)), ((), ())), preferred_element_type=jnp.float32
    )


def dot_nt(left, right):
    return lax.dot_general(
        left, right, (((1,), (1,)), ((), ())), preferred_element_type=jnp.float32
    )


def kernel(
    n,
    corr_hbm,
    points_hbm,
    levels_hbm,
    codes_hbm,
    map_hbm,
    slab_hbm,
    coef_ref,
    narrow_ref,
    permuted,
    packets,
    norms_all,
    points_all,
    corr_ref,
    points_ref,
    levels_ref,
    codes_ref,
    map_ref,
    weights,
    blocks,
    table,
    design,
    total,
    total_in,
    fitted,
    outgoing,
    summed,
    codes,
    cells,
    squares_ref,
    slab,
    local_sem,
    packets_send,
    packets_recv,
    relay_send,
    relay_recv,
    blocks_send,
    blocks_recv,
    total_send,
    total_recv,
    summed_send,
    summed_recv,
):
    me = lax.axis_index("runs")
    chips = n // 2
    chip = me // 2
    core = lax.rem(me, 2)
    terms, modes = corr_ref.shape
    width = modes // chips
    runs = table.shape[1]
    half = table.shape[0] // 2
    side = chips // 2
    low_side = chip < side
    inner = jnp.logical_and(chip >= side // 2, chip < chips - side // 2)

    def chip_at(offset):
        return lax.rem(chip + offset, chips)

    def near_chip(step):
        base = chip // side * side
        return base + lax.rem(chip - base + step, side)

    def far_chip(step):
        row = step // 2
        row = jnp.where(low_side, side - 1 - row, row)
        return 2 * row + lax.rem(chip + 1 + step, 2)

    def offset_to(there):
        return lax.rem(there - chip + chips, chips)

    def term_rows(index):
        return pl.ds(pl.multiple_of(index * terms, terms), terms)

    def mode_lanes(index):
        return pl.ds(pl.multiple_of(index * width, width), width)

    def remote(src, dst, send, recv, target):
        return pltpu.make_async_remote_copy(
            src_ref=src,
            dst_ref=dst,
            send_sem=send,
            recv_sem=recv,
            device_id={"runs": target},
            device_id_type=pl.DeviceIdType.MESH,
        )

    barrier = pltpu.get_barrier_semaphore()
    peers = [chip_at(offset) * 2 + core for offset in range(1, chips)]
    for there in [*peers, chip * 2 + (1 - core)]:
        pl.semaphore_signal(
            barrier,
            inc=1,
            device_id={"runs": there},
            device_id_type=pl.DeviceIdType.MESH,
        )

    copies = [
        pltpu.make_async_copy(src, dst, local_sem.at[index])
        for index, (src, dst) in enumerate(
            [
                (corr_hbm, corr_ref),
                (points_hbm, points_ref),
                (levels_hbm, levels_ref),
                (codes_hbm, codes_ref),
                (map_hbm, map_ref),
                (slab_hbm, slab),
            ]
        )
    ]
    slab_copy = copies[-1]
    own_copy = pltpu.make_async_copy(
        corr_ref.at[:, mode_lanes(chip)],
        blocks.at[term_rows(chip)],
        local_sem.at[len(copies)],
    )
    for copy in copies:
        copy.start()
    for copy in copies[:2]:
        copy.wait()
    own_copy.start()

    wide = corr_ref[...].astype(jnp.float32)
    squares = wide * wide
    high = squares.astype(jnp.bfloat16)
    low = (squares - high.astype(jnp.float32)).astype(jnp.bfloat16)
    ones = jnp.ones((8, modes), jnp.bfloat16)
    norm_rows = dot_nt(ones, high) + dot_nt(ones, low)
    inputs = points_ref.shape[0]
    fold = inputs // 2
    norm_lanes = [
        (fold + start // LANES, slice(start, start + LANES))
        for start in range(0, terms, LANES)
    ]
    packets[core, chip, 0:fold] = jnp.concatenate(
        [points_ref[0:fold], points_ref[fold:inputs]], axis=1
    )
    for row, lanes in norm_lanes:
        packets[core, chip, row : row + 1] = norm_rows[0:1, lanes]
    pl.semaphore_wait(barrier, chips)

    def packet_move(offset):
        return remote(
            packets.at[core, chip],
            packets.at[core, chip],
            packets_send,
            packets_recv.at[offset],
            chip_at(offset) * 2 + core,
        )

    def block_move(offset):
        there = chip_at(offset)
        return remote(
            corr_ref.at[:, mode_lanes(there)],
            blocks.at[term_rows(chip)],
            blocks_send,
            blocks_recv.at[offset],
            there * 2 + core,
        )

    def relay():
        mine = packets.at[core]
        return remote(mine, mine, relay_send, relay_recv, chip * 2 + (1 - core))

    def total_move():
        return remote(total, total_in, total_send, total_recv, chip * 2 + (1 - core))

    def summed_move(offset):
        there = chip_at(offset)
        return remote(
            outgoing.at[term_rows(there)],
            summed.at[:, mode_lanes(chip)],
            summed_send,
            summed_recv.at[offset],
            there * 2 + core,
        )

    targets = [far_chip(step) for step in range(side)]
    targets += [near_chip(step) for step in range(1, side)]
    for there in targets:
        packet_move(offset_to(there)).start()
    def send_far():
        for step in range(side):
            block_move(offset_to(far_chip(step))).start()

    pl.when(inner)(send_far)
    for step in range(1, side):
        block_move(offset_to(near_chip(step))).start()

    for copy in copies[2:-1]:
        copy.wait()
    for index in range(n):
        weights[index % 2, index // 2] = jnp.exp2(
            levels_ref[index].astype(jnp.float32)
        )

    for index in range(chips):
        lanes = term_rows(index * 2 + core)
        code = codes_ref[:, lanes]
        position = lax.shift_right_logical(code * 205, 10)
        code = (code - DEGREES * position) * inputs + position
        spare = jnp.zeros((8 - code.shape[0], terms), jnp.int32)
        codes[index * terms : (index + 1) * terms, :] = jnp.transpose(
            jnp.concatenate([code, spare], axis=0)
        )

    for start in range(0, map_ref.shape[1], 256):
        lanes = slice(start, start + 256)
        cells[lanes, :] = jnp.transpose(
            jnp.broadcast_to(map_ref[:, lanes], (8, 256))
        )

    pl.when(jnp.logical_not(inner))(send_far)

    place = lax.broadcasted_iota(jnp.int32, (256, slab.shape[0]), 1)
    chunks = cells.shape[0] // 256
    early, middle = chunks // 8, chunks // 4

    def permute(first, last):
        @pl.loop(first, last)
        def _(step):
            rows = pl.ds(pl.multiple_of(step * 256, 256), 256)
            pick = jnp.where(place == cells[rows, 0:1], 1.0, 0.0).astype(jnp.bfloat16)
            permuted[rows, :] = dot_nn(pick, slab[...]).astype(jnp.bfloat16)

    slab_copy.wait()
    permute(0, early)
    for offset in range(1, chips):
        packet_move(offset).wait_recv()
    packets_relay = relay()
    packets_relay.start()
    permute(early, middle)
    packets_relay.wait_recv()
    first_core = lax.broadcasted_iota(jnp.int32, (fold, LANES), 1) < LANES // 2
    for index in range(chips):
        even, odd = (packets[side, index, 0:fold] for side in range(2))
        turned = pltpu.roll(odd, LANES // 2, 1)
        points_all[index, 0:fold] = jnp.where(first_core, even, turned)
        turned = pltpu.roll(even, LANES // 2, 1)
        points_all[index, fold:inputs] = jnp.where(first_core, turned, odd)
        for which in range(2):
            for row, lanes in norm_lanes:
                norms_all[which, index, :, lanes] = packets[which, index, row : row + 1]
    for index in range(chips):
        points = points_all[index]
        columns = hermite_columns(points)
        used = DEGREES * points.shape[0]
        if used < half:
            columns.append(jnp.zeros((half - used, points.shape[1]), jnp.float32))
        values = jnp.concatenate(columns, axis=0)
        upper = values.astype(jnp.bfloat16)
        lower = (values - upper.astype(jnp.float32)).astype(jnp.bfloat16)
        lanes = slice(index * points.shape[1], (index + 1) * points.shape[1])
        table[0:half, lanes] = upper
        table[half:, lanes] = lower

    ratio = jnp.sqrt(norms_all[...]) / weights[...]
    penalty = LAMBDA_FRACTION * jnp.max(
        jnp.max(jnp.max(ratio, axis=0), axis=0), axis=1, keepdims=True
    )
    own_copy.wait()
    total[...] = jnp.zeros_like(total)
    position = lax.broadcasted_iota(jnp.int32, (terms, 2 * half), 1)
    position = jnp.where(position >= half, position - half, position)
    piece = min(256, runs)

    def build(there):
        rows = term_rows(there)
        picks = [
            jnp.where(position == codes[rows, slot : slot + 1], 1.0, 0.0).astype(
                jnp.bfloat16
            )
            for slot in range(codes_ref.shape[0])
        ]
        for start in range(0, runs, piece):
            lanes = slice(start, start + piece)
            product = dot_nn(picks[0], table[:, lanes])
            for pick in picks[1:]:
                product = product * dot_nn(pick, table[:, lanes])
            design[rows, lanes] = product.astype(jnp.bfloat16)

    def fit(there):
        rows = term_rows(there)
        length = jnp.sqrt(STEP * STEP * norms_all[core, there] + EPSILON)
        limits = STEP * penalty * weights[core, there]
        factor = jnp.maximum(0.0, 1.0 - limits / length)
        turned = jnp.transpose(blocks[rows, :].astype(jnp.float32))
        first_half = (STEP * turned * factor).astype(jnp.bfloat16)
        total[...] += dot_nn(first_half, design[rows, :])

    def wait_block(there):
        block_move(lax.rem(chip - there + chips, chips)).wait_recv()

    @pl.loop(0, chips, unroll=2)
    def _(step):
        build(step)

    fit(chip)
    for step in range(1, side):
        wait_block(near_chip(step))
        fit(near_chip(step))
    filled = jnp.where(inner, middle + 1, middle)
    permute(middle, filled)
    for step in range(side):
        wait_block(far_chip(step))
        fit(far_chip(step))

    total_move().start()
    total_move().wait_recv()
    fitted[...] = (total[...] + total_in[...]).astype(jnp.bfloat16)

    @pl.loop(1, chips)
    def _(step):
        there = jnp.where(
            step <= side, far_chip(lax.min(step, side) - 1), near_chip(step - side)
        )
        rows = term_rows(there)
        outgoing[rows, :] = dot_nt(design[rows, :], fitted[...]).astype(jnp.bfloat16)
        summed_move(offset_to(there)).start()

    summed[:, mode_lanes(chip)] = dot_nt(
        design[term_rows(chip), :], fitted[...]
    ).astype(jnp.bfloat16)

    permute(filled, chunks)
    own_limits = jnp.broadcast_to(STEP * penalty * weights[core, chip], (8, terms))
    limits = jnp.transpose(own_limits)[:, 0:1]
    chunk = 32
    for start in range(0, terms, chunk):
        rows = slice(start, start + chunk)
        half_corr = STEP * corr_ref[rows].astype(jnp.float32)
        coef_ref[rows] = shrink(half_corr, limits[rows]) + half_corr
    def subtract(there):
        lanes = mode_lanes(there)
        values = coef_ref[:, lanes] - summed[:, lanes].astype(jnp.float32) * (
            STEP / runs
        )
        coef_ref[:, lanes] = values
        squares = values * values
        parts = [squares[:, at : at + LANES] for at in range(0, width, LANES)]
        return functools.reduce(jnp.add, parts)

    squares_ref[...] = subtract(chip)
    arrivals = [near_chip(step) for step in range(1, side)]
    arrivals += [far_chip(step) for step in range(side)]
    for there in arrivals:
        summed_move(lax.rem(chip - there + chips, chips)).wait_recv()
        squares_ref[...] += subtract(there)
    length = jnp.sqrt(jnp.sum(squares_ref[...], axis=1, keepdims=True) + EPSILON)
    factor = jnp.maximum(0.0, 1.0 - limits / length)
    for start in range(0, terms, chunk):
        rows = slice(start, start + chunk)
        coefficients = coef_ref[rows] * factor[rows]
        coef_ref[rows] = coefficients
        narrow_ref[rows] = coefficients.astype(jnp.bfloat16)

    packets_relay.wait_send()
    total_move().wait_send()
    others = chips - 1
    partner = chip * 2 + (1 - core)
    sent = packets.at[core, 0:others]
    remote(sent, sent, packets_send, relay_recv, partner).wait_send()
    sent = outgoing.at[0 : others * terms]
    remote(sent, sent, blocks_send, relay_recv, partner).wait_send()
    remote(sent, sent, summed_send, relay_recv, partner).wait_send()


def finish(coef_in, narrow, permuted, coef_hbm, lift_hbm, lift, sems):
    copies = [pltpu.make_async_copy(coef_in, coef_hbm, sems.at[0])]
    copies[0].start()
    parts, _, width = lift.shape
    for part in range(parts):
        lanes = slice(part * width, (part + 1) * width)
        lift[part] = dot_nt(narrow[...], permuted[lanes]).astype(jnp.bfloat16)
        copy = pltpu.make_async_copy(
            lift.at[part], lift_hbm.at[:, lanes], sems.at[part + 1]
        )
        copy.start()
        copies.append(copy)
    for copy in copies:
        copy.wait()


def by_chips(run_inputs, term_codes, weight_levels, correlations, slab_modes, cell_map):
    run_count, inputs = run_inputs.shape
    terms, modes = correlations.shape
    n = lax.axis_size("runs")
    chips = n // 2
    runs = run_count * n
    count = cell_map.shape[0]
    width = modes // chips
    lane_terms = chips * terms
    packet = -(-(inputs // 2 + terms // LANES) // 8) * 8
    half = -(-DEGREES * inputs // LANES) * LANES
    f32, bf16 = jnp.float32, jnp.bfloat16
    vmem = pl.BlockSpec(memory_space=pltpu.VMEM)
    hbm = pl.BlockSpec(memory_space=pltpu.HBM)
    dma = pltpu.SemaphoreType.DMA
    *solved, permuted = pl.pallas_call(
        functools.partial(kernel, n),
        out_shape=(
            jax.ShapeDtypeStruct((terms, modes), f32),
            jax.ShapeDtypeStruct((terms, modes), bf16),
            jax.ShapeDtypeStruct((count, modes), bf16),
        ),
        in_specs=[hbm] * 6,
        out_specs=(vmem, vmem, vmem),
        scratch_shapes=[
            pltpu.VMEM((2, chips, packet, LANES), f32),
            pltpu.VMEM((2, chips, 1, terms), f32),
            pltpu.VMEM((chips, inputs, LANES), f32),
            pltpu.VMEM((terms, modes), bf16),
            pltpu.VMEM((inputs, run_count), f32),
            pltpu.VMEM((n, 1, terms), jnp.int32),
            pltpu.VMEM((term_codes.shape[1], n * terms), jnp.int32),
            pltpu.VMEM((1, count), jnp.int32),
            pltpu.VMEM((2, chips, 1, terms), f32),
            pltpu.VMEM((lane_terms, width), bf16),
            pltpu.VMEM((2 * half, runs), bf16),
            pltpu.VMEM((lane_terms, runs), bf16),
            pltpu.VMEM((width, runs), f32),
            pltpu.VMEM((width, runs), f32),
            pltpu.VMEM((width, runs), bf16),
            pltpu.VMEM((lane_terms, width), bf16),
            pltpu.VMEM((terms, modes), bf16),
            pltpu.VMEM((lane_terms, 8), jnp.int32),
            pltpu.VMEM((count, 8), jnp.int32),
            pltpu.VMEM((terms, LANES), f32),
            pltpu.VMEM(slab_modes.shape, bf16),
            dma((7,)),
            dma,
            dma((chips,)),
            dma,
            dma,
            dma,
            dma((chips,)),
            dma,
            dma,
            dma,
            dma((chips,)),
        ],
        compiler_params=pltpu.CompilerParams(
            collective_id=0, has_side_effects=True, vmem_limit_bytes=40 * 2**20
        ),
    )(
        *[
            pltpu.with_memory_space_constraint(array, pltpu.HBM)
            for array in (
                correlations,
                run_inputs.T,
                weight_levels.reshape(n, 1, terms),
                term_codes.T,
                cell_map.reshape(1, count),
                slab_modes,
            )
        ]
    )
    width = 512
    parts = count // width
    return pl.pallas_call(
        finish,
        out_shape=(
            jax.ShapeDtypeStruct((terms, modes), f32),
            jax.ShapeDtypeStruct((terms, count), bf16),
        ),
        in_specs=[vmem, vmem, vmem],
        out_specs=(hbm, hbm),
        scratch_shapes=[
            pltpu.VMEM((parts, terms, width), bf16),
            dma((parts + 1,)),
        ],
        compiler_params=pltpu.CompilerParams(vmem_limit_bytes=8 * 2**20),
    )(*solved, permuted)


def by_gathers(
    run_inputs, term_codes, weight_levels, correlations, slab_modes, cell_map
):
    run_count = run_inputs.shape[0]
    term_count = correlations.shape[0]
    devices = lax.axis_size("runs")
    offset = lax.axis_index("runs") * term_count
    total_runs = run_count * devices
    weights_all = jnp.exp2(weight_levels.astype(jnp.float32))
    own_weights = lax.dynamic_slice_in_dim(weights_all, offset, term_count)
    own_corr = correlations.astype(jnp.float32)
    ratio = jnp.max(jnp.sqrt(jnp.sum(own_corr * own_corr, axis=1)) / own_weights)
    penalty = LAMBDA_FRACTION * lax.pmax(ratio, "runs")
    limits = (STEP * penalty * own_weights)[:, None]
    first = shrink(STEP * own_corr, limits)
    design = basis(run_inputs, term_codes)
    fitted = dot_nn(
        design,
        lax.all_gather(first.astype(jnp.bfloat16), "runs", axis=0, tiled=True),
    )
    fitted_half = fitted.astype(jnp.bfloat16)
    all_points = lax.all_gather(run_inputs, "runs", axis=0, tiled=True)
    own_codes = lax.dynamic_slice_in_dim(term_codes, offset, term_count, 0)
    owned_design = basis(all_points, own_codes)
    summed = lax.dot_general(
        owned_design,
        lax.all_gather(fitted_half, "runs", axis=0, tiled=True),
        (((0,), (0,)), ((), ())),
        preferred_element_type=jnp.float32,
    )
    gradient = summed / total_runs - own_corr
    coefficients = shrink(first - STEP * gradient, limits)
    modes = jnp.take(slab_modes, cell_map, axis=0)
    lifted = dot_nt(coefficients.astype(jnp.bfloat16), modes).astype(jnp.bfloat16)
    return (coefficients, lifted)


def on_device(run_inputs, term_codes, weight_levels, correlations, slab_modes, cell_map):
    n = lax.axis_size("runs")
    terms, modes = correlations.shape
    aligned = (
        n % 8 == 0
        and modes % (LANES * max(n // 2, 1)) == 0
        and terms % LANES == 0
        and term_codes.shape[1] <= 8
        and DEGREES * run_inputs.shape[1] < 1024
        and 2 * run_inputs.shape[0] == LANES
        and run_inputs.shape[1] % 8 == 0
        and cell_map.shape[0] % 512 == 0
        and (run_inputs.shape[0] * n) % 256 == 0
    )
    step = by_chips if aligned else by_gathers
    return step(
        run_inputs, term_codes, weight_levels, correlations, slab_modes, cell_map
    )


def solution(mesh):
    return jax.shard_map(
        on_device,
        mesh=mesh,
        in_specs=(
            P(("cases", "runs"), None),
            P(),
            P(),
            P(("cases", "runs"), None),
            P("cases", None),
            P(),
        ),
        out_specs=(P(("cases", "runs"), None), P(("cases", "runs"), None)),
        check_vma=False,
    )
```
